128 devices in a mesh: leaf: 8 (over z, x_hi), ctx: 16 (over y, x_lo, core).
Axes of the slice: x: 4 (x_hi: 2, x_lo: 2; x = x_hi * 2 + x_lo), y: 4, z: 4, core: 2. Of those that a mesh axis runs over, the one named last changes fastest.
Arguments:
- queries: bfloat16 [16384, 8192], P(('leaf', 'ctx')), may hold values from -38 to 38, as said below
- seg_keys: bfloat16 [16384, 1024], P(('leaf', 'ctx')), may hold values from -6 to 6
- seg_values: bfloat16 [16384, 1024], P(('leaf', 'ctx')), may hold values from -6 to 6
- root_keys: bfloat16 [2048, 1024], P('ctx'), may hold values from -6 to 6, as said below
- root_values: bfloat16 [2048, 1024], P('ctx'), may hold values from -6 to 6
- expansion: int32 [2, 8], replicated, may hold values from 0 to 7, as said below
- root_offsets: int32 [8], replicated, may hold values from 512 to 2048
Outputs:
- attended: bfloat16 [16384, 8192], P(('leaf', 'ctx'))
The draws below stay inside these ranges and needn't reach their ends.
Inputs may be any that keep to these rules, and one draw needn't show every extreme that they name: queries of order one, with some rows much larger. `root_keys`: keys of order one. `expansion`: group 8 - 1 is the root: it has depth 0 and is its own parent; every other group's parent has depth one less than its own.
All inputs are finite; a program needn't handle non-finite values.
Results may differ from the reference program's by a relative error of at most 0.0065.
Values may be sent and summed in bfloat16 or wider, within the bound.
A program may use at most 128 MiB of HBM per device.

```python
import math
import jax
import jax.numpy as jnp
from jax import lax

HQ = 64
KVH = 8
HD = 128
GROUPS = 8
SEG = 2048
L_ROOT = 2048


def root_table(key):
    table_key = jax.random.fold_in(key, 101)
    key_table = jnp.clip(jax.random.normal(table_key, (L_ROOT, KVH * HD), jnp.float32), -6.0, 6.0)
    return key_table


def draw_root_keys(key, part):
    return root_table(key).astype(jnp.bfloat16)


def draw_queries(key, part):
    query_key = jax.random.fold_in(key, 202)
    total_rows = GROUPS * SEG
    drawn = jnp.clip(jax.random.normal(query_key, (total_rows, HQ * HD), jnp.float32), -6.0, 6.0)
    return drawn.astype(jnp.bfloat16)


def draw_expansion(key, part):
    key_order = jax.random.fold_in(key, 303)
    key_picks = jax.random.fold_in(key, 304)
    later_order = jax.random.permutation(key_order, GROUPS - 1).astype(jnp.int32)
    visit_order = jnp.concatenate([jnp.full((1,), GROUPS - 1, jnp.int32), later_order]).astype(jnp.int32)
    raw_picks = jax.random.randint(key_picks, (GROUPS,), 0, 1 << 20).astype(jnp.int32)
    parents = jnp.zeros((GROUPS,), jnp.int32).at[visit_order[0]].set(visit_order[0])
    depths = jnp.zeros((GROUPS,), jnp.int32)
    for position in range(1, GROUPS):
        parent_id = visit_order[raw_picks[position] % position]
        parents = parents.at[visit_order[position]].set(parent_id)
        depths = depths.at[visit_order[position]].set(depths[parent_id] + 1)
    return jnp.stack([parents, depths]).astype(jnp.int32)


def with_ends(values, stream_key, least, high):
    longest = values.shape.index(max(values.shape))
    spots = []
    for shift in (0, 1):
        where = [jax.random.randint(jax.random.fold_in(stream_key, axis), (), 0, length) for axis, length in enumerate(values.shape)]
        where[longest] = (where[longest] + shift) % values.shape[longest]
        spots.append(tuple(where))
    return values.at[spots[0]].set(least).at[spots[1]].set(high)


def steps_of(rng, extent, shards, low, high):
    gain, own = 1.0, jax.random.fold_in(rng, 6)
    for dim, parts in shards:
        steps = jnp.exp(jax.random.uniform(jax.random.fold_in(own, dim), (parts,), jnp.float32, low / len(shards), high / len(shards)))
        gain = gain * jnp.repeat(steps, extent[dim] // parts).reshape([-1 if axis == dim else 1 for axis in range(len(extent))])
    return gain


def centred(own_key, shape, deviation, reach, pieces=(), held_as=jnp.bfloat16):
    loudness = steps_of(own_key, shape, pieces, -0.22, 0.18) if pieces else 1.0
    array = jax.random.normal(own_key, shape, jnp.float32) * deviation * loudness
    return jnp.minimum(jnp.maximum(array, -reach), reach).astype(held_as)


def setup_inputs(seed: int = 0) -> dict:
    seeds = jax.random.split(jax.random.key(seed), 8)
    return {
        "queries": draw_queries(jax.random.fold_in(seeds[7], 71), 0),
        "seg_keys": centred(seeds[1], (GROUPS * SEG, KVH * HD), 1.0, 6.0, ((0, 128),)),
        "seg_values": centred(seeds[2], (GROUPS * SEG, KVH * HD), 1.0, 6.0, ((0, 128),)),
        "root_keys": draw_root_keys(jax.random.fold_in(seeds[7], 71), 0),
        "root_values": centred(seeds[4], (L_ROOT, KVH * HD), 1.0, 6.0, ((0, 16),)),
        "expansion": draw_expansion(jax.random.fold_in(seeds[7], 71), 0),
        "root_offsets": with_ends(jax.random.randint(seeds[6], (GROUPS,), L_ROOT // 4, L_ROOT + 1), jax.random.fold_in(seeds[6], 1), L_ROOT // 4, L_ROOT).astype(jnp.int32),
    }


def reference(queries, seg_keys, seg_values, root_keys, root_values, expansion, root_offsets):
    group_width = HQ // KVH
    score_scale = 1.0 / math.sqrt(HD)
    query_pos = jnp.arange(SEG, dtype=jnp.int32)
    key_index = jnp.arange(L_ROOT + 2 * SEG, dtype=jnp.int32)
    in_root = key_index < L_ROOT
    in_parent = (key_index >= L_ROOT) & (key_index < L_ROOT + SEG)
    own_pos = key_index - L_ROOT - SEG

    def one_pair(pair_index):
        group_idx = (pair_index // KVH).astype(jnp.int32)
        head_index = (pair_index % KVH).astype(jnp.int32)
        parent = expansion[0, group_idx].astype(jnp.int32)
        tree_depth = expansion[1, group_idx]
        visible = root_offsets[group_idx]
        head_query = lax.dynamic_slice(queries, (group_idx * SEG, head_index * group_width * HD), (SEG, group_width * HD)).reshape(SEG, group_width, HD)
        zero_row = jnp.zeros((), jnp.int32)
        all_keys = jnp.concatenate([lax.dynamic_slice(root_keys, (zero_row, head_index * HD), (L_ROOT, HD)), lax.dynamic_slice(seg_keys, (parent * SEG, head_index * HD), (SEG, HD)), lax.dynamic_slice(seg_keys, (group_idx * SEG, head_index * HD), (SEG, HD))], axis=0)
        all_values = jnp.concatenate([lax.dynamic_slice(root_values, (zero_row, head_index * HD), (L_ROOT, HD)), lax.dynamic_slice(seg_values, (parent * SEG, head_index * HD), (SEG, HD)), lax.dynamic_slice(seg_values, (group_idx * SEG, head_index * HD), (SEG, HD))], axis=0)
        scores = jnp.einsum('qgd,kd->gqk', head_query.astype(jnp.float32), all_keys.astype(jnp.float32)) * score_scale
        allowed = (in_root & (key_index < visible))[None, :] | (in_parent & (tree_depth > 0))[None, :] | (own_pos >= 0)[None, :] & (own_pos[None, :] <= query_pos[:, None])
        masked = jnp.where(allowed[None], scores, -jnp.inf)
        row_max = lax.optimization_barrier(jnp.max(masked, axis=-1, keepdims=True))
        weights = jnp.where(allowed[None], jnp.exp(masked - row_max), 0.0)
        row_total = lax.optimization_barrier(jnp.sum(weights, axis=-1))
        rounded = lax.optimization_barrier(weights.astype(jnp.bfloat16))
        blended = jnp.einsum('gqk,kd->gqd', rounded.astype(jnp.float32), all_values.astype(jnp.float32))
        return blended / row_total[..., None]
    stacked = lax.map(one_pair, jnp.arange(GROUPS * KVH, dtype=jnp.int32))
    stacked = stacked.reshape(GROUPS, KVH, group_width, SEG, HD).transpose(0, 3, 1, 2, 4).reshape(GROUPS * SEG, HQ * HD)
    return stacked.astype(jnp.bfloat16)
```

```python
import functools
import math

import jax
import jax.numpy as jnp
from jax import lax
from jax.experimental import pallas as pl
from jax.experimental.pallas import tpu as pltpu
from jax.sharding import PartitionSpec as P

HQ = 64
KVH = 8
HD = 128
MESH = pl.DeviceIdType.MESH
SCALE = math.log2(math.e) / math.sqrt(HD)
LOW = -1e30

ROOT, OWN, PAR = 0, 1, 2
ORDERS = ((0, 1, 2), (1, 2, 0), (2, 0, 1))


def order_of(source, part):
    return ORDERS[part] if part < 3 else ORDERS[source]


N_PARTNER = 9
N_STEP = 36
N_LEAF = 5
N_OUT = 4
BASE_STEP = N_PARTNER
BASE_LEAF = BASE_STEP + N_STEP
BASE_OUT = BASE_LEAF + N_LEAF
N_COPIES = BASE_OUT + N_OUT
N_LOCAL = 14
KB = 1024
RB = 512


def kernel(expansion, offsets, q_hbm, k_hbm, v_hbm, rk_hbm, rv_hbm, o_hbm,
           kv, qbuf, zbuf, pick, got, acc, top, den, bound, stage, send_sem, recv_sem, local_sem):
    leaf, ctx = lax.axis_index("leaf"), lax.axis_index("ctx")
    z, xh = leaf // 2, leaf % 2
    y, c, k = ctx // 4, (ctx // 2) % 2, ctx % 2
    a, b = ((y + 1) // 2) % 2, y // 2
    d, e = ((z + 1) // 2) % 2, z // 2
    partner = (leaf, ctx + 1 - 2 * k)
    near = (
        (leaf, ctx + 4 - 8 * (y % 2)),
        (leaf, (3 - y) * 4 + c * 2 + k),
        (leaf, ctx + 2 - 4 * c),
    )
    near_d = ((z + 1 - 2 * (z % 2)) * 2 + xh, ctx)
    near_e = ((3 - z) * 2 + xh, ctx)
    near_f = (leaf + 1 - 2 * xh, ctx + 2 - 4 * c)

    barrier = pltpu.get_barrier_semaphore()
    for other in (partner, *near, near_d, near_e, near_f):
        pl.semaphore_signal(barrier, inc=1, device_id=other, device_id_type=MESH)
    pl.semaphore_wait(barrier, 7)

    def remote(src, dst, number, device):
        return pltpu.make_async_remote_copy(
            src_ref=src, dst_ref=dst, send_sem=send_sem.at[number], recv_sem=recv_sem.at[number],
            device_id=device, device_id_type=MESH,
        )

    mine512 = pl.ds(pl.multiple_of(k * 512, 128), 512)
    other512 = pl.ds(pl.multiple_of((1 - k) * 512, 128), 512)
    mine4096 = pl.ds(pl.multiple_of(k * 4096, 128), 4096)
    other4096 = pl.ds(pl.multiple_of((1 - k) * 4096, 128), 4096)
    mine128 = pl.ds(pl.multiple_of(k * 128, 128), 128)
    other128 = pl.ds(pl.multiple_of((1 - k) * 128, 128), 128)

    def pair_copies(source, number, arrays):
        sends, locals_ = [], []
        for t, array in enumerate(arrays):
            for j in range(2):
                rows = pl.ds(64 * j, 64)
                slot = kv.at[source, 2 * k + j, a, b, c, t]
                n = number + 2 * t + j
                sends.append(remote(array.at[rows, other512], slot, n, partner))
                locals_.append(pltpu.make_async_copy(array.at[rows, mine512], slot, local_sem.at[n]))
        return sends, locals_

    root_sends, root_locals = pair_copies(ROOT, 0, (rk_hbm, rv_hbm))
    own_sends, own_locals = pair_copies(OWN, 4, (k_hbm, v_hbm))
    q_send = remote(q_hbm.at[:, other4096], qbuf.at[mine128, :], 8, partner)
    q_local = pltpu.make_async_copy(q_hbm.at[:, mine4096], qbuf.at[mine128, :], local_sem.at[8])
    for copy in (*root_sends, *root_locals, *own_sends, *own_locals, q_send, q_local):
        copy.start()

    bits = (a, b, c)

    def step_copies(source, step):
        copies = []
        for part in range(4):
            order = order_of(source, part)
            have = order[:step]
            where = [slice(None) if dim in have else bits[dim] for dim in range(3)]
            slot = kv.at[source, part, where[0], where[1], where[2]]
            n = BASE_STEP + source * 12 + step * 4 + part
            copies.append(remote(slot, slot, n, near[order[step]]))
        return copies

    steps = {(s, t): step_copies(s, t) for s in range(3) for t in range(3)}

    def start(copies):
        for copy in copies:
            copy.start()

    def arrive(copies):
        for copy in copies:
            copy.wait_recv()

    def wait_all(copies):
        for copy in copies:
            copy.wait()

    leaf1 = [
        remote(kv.at[OWN, 0:2, a, b, c], zbuf.at[d, e, 0:2], BASE_LEAF, near_d),
        remote(kv.at[OWN, 2:4, a, b, c], zbuf.at[d, e, 2:4], BASE_LEAF + 1, near_e),
    ]
    leaf_local = pltpu.make_async_copy(kv.at[OWN, :, a, b, c], zbuf.at[d, e], local_sem.at[9])
    leaf2 = [
        remote(zbuf.at[:, e, 0:2], zbuf.at[:, e, 0:2], BASE_LEAF + 2, near_e),
        remote(zbuf.at[d, :, 2:4], zbuf.at[d, :, 2:4], BASE_LEAF + 3, near_d),
    ]
    leaf3 = [remote(pick, got, BASE_LEAF + 4, near_f)]

    arrive(root_sends)
    wait_all(root_locals)
    start(steps[ROOT, 0])
    arrive(own_sends)
    wait_all(own_locals)
    start(leaf1)
    start(steps[OWN, 0])
    leaf_local.start()

    acc[...] = jnp.zeros(acc.shape, jnp.float32)
    den[...] = jnp.zeros(den.shape, jnp.float32)
    top[...] = jnp.full(top.shape, LOW, jnp.float32)

    arrive(steps[ROOT, 0])
    start(steps[ROOT, 1])
    arrive(steps[OWN, 0])
    start(steps[OWN, 1])
    leaf_local.wait()
    arrive(leaf1)
    start(leaf2)
    arrive([q_send])
    q_local.wait()
    arrive(steps[ROOT, 1])
    start(steps[ROOT, 2])

    parent, depth, visible = expansion[0, leaf], expansion[1, leaf], offsets[leaf]
    parent_f = expansion[0, near_f[0]]
    row_pos = y * 512 + c * 256

    def unit_of(group, part, t):
        zg = group // 2
        return zbuf[((zg + 1) // 2) % 2, zg // 2, part, t]

    def choose_for_f():
        for part in range(4):
            for t in range(2):
                pick[part, t] = unit_of(parent_f, part, t)

    def choose_parent():
        here = (parent % 2) == xh
        for part in range(4):
            for t in range(2):
                kv[PAR, part, a, b, c, t] = jnp.where(here, unit_of(parent, part, t), got[part, t])

    out_cols = [pl.ds(pl.multiple_of((k * 4 + h) * 1024, 128), 1024) for h in range(4)]
    back_cols = [pl.ds(pl.multiple_of(((1 - k) * 4 + h) * 1024, 128), 1024) for h in range(4)]
    out_sends = [
        remote(stage.at[other128, h * 1024:(h + 1) * 1024], o_hbm.at[:, out_cols[h]], BASE_OUT + h, partner)
        for h in range(4)
    ]
    out_locals = [
        pltpu.make_async_copy(stage.at[mine128, h * 1024:(h + 1) * 1024], o_hbm.at[:, out_cols[h]], local_sem.at[10 + h])
        for h in range(4)
    ]

    def send_head(h):
        out_sends[h].start()
        out_locals[h].start()

    hooks = {
        1: lambda: (arrive(steps[OWN, 1]), start(steps[OWN, 2])),
        2: lambda: (arrive(leaf2), choose_for_f()),
        3: lambda: start(leaf3),
        4: lambda: arrive(steps[ROOT, 2]),
        7: lambda: (arrive(leaf3), choose_parent()),
        8: lambda: (start(steps[PAR, 0]), arrive(steps[OWN, 2])),
        10: lambda: (arrive(steps[PAR, 0]), start(steps[PAR, 1])),
        13: lambda: (arrive(steps[PAR, 1]), start(steps[PAR, 2])),
        20: lambda: arrive(steps[PAR, 2]),
        21: lambda: send_head(0),
        22: lambda: send_head(1),
        23: lambda: send_head(2),
    }

    lane = lax.broadcasted_iota(jnp.int32, (1, 128), 1)

    def one(it, carry):
        for number, act in hooks.items():
            @pl.when(it == number)
            def _():
                act()
        chunk, h = it // 4, it % 4
        source, half = chunk // 2, chunk % 2
        is_own = source == OWN
        columns = pl.ds(pl.multiple_of(h * HD, HD), HD)

        pieces = []
        for part in range(4):
            lasts = [order_of(s, part)[2] for s in range(3)]
            fixed = jnp.where(is_own, 1, jnp.where(source == ROOT, lasts[ROOT], lasts[PAR]))
            own_bit = jnp.where(fixed == 0, a, jnp.where(fixed == 1, b, c))
            bit = jnp.where(is_own, half, (own_bit + half) % 2)
            for j in range(4):
                j1, j0 = j // 2, j % 2
                pa = jnp.where(fixed == 0, bit, j1)
                pb = jnp.where(fixed == 1, bit, jnp.where(fixed == 0, j1, j0))
                pc = jnp.where(fixed == 2, bit, j0)
                plane = 2 * pb + pa + pb - 2 * pa * pb
                pieces.append((part, pa, pb, pc, plane * 512 + pc * 256 + part * 64))

        @pl.when(h == 0)
        def _():
            limit = jnp.where(source == ROOT, visible, jnp.where(depth > 0, 4096, 0))
            rows = lax.broadcasted_iota(jnp.int32, (256, 1), 0) + row_pos + 1
            limits = jnp.where(is_own, rows, limit)
            for j in range(8):
                base = jnp.where(lane < 64, pieces[2 * j][4] + lane, pieces[2 * j + 1][4] + lane - 64)
                bound[:, j * 128:(j + 1) * 128] = jnp.where(base < limits, 1e38, LOW)

        keys = jnp.concatenate([kv[source, p, pa, pb, pc, 0, :, columns] for p, pa, pb, pc, _ in pieces], 0)
        values = jnp.concatenate([kv[source, p, pa, pb, pc, 1, :, columns] for p, pa, pb, pc, _ in pieces], 0)
        values = jnp.concatenate([values, jnp.ones((KB, HD), jnp.bfloat16)], 1)

        def score(sb):
            rows = [
                qbuf[:, pl.ds(pl.multiple_of((h * 8 + 2 * sb + i) * HD, HD), HD)] for i in range(2)
            ]
            return lax.dot_general(
                jnp.concatenate(rows, 0), keys, (((1,), (1,)), ((), ())), preferred_element_type=jnp.float32
            )

        def soften(sb, s):
            rows = pl.ds(sb * RB, RB)
            old = top[h, rows, :]
            limited, best = [], None
            for j in range(KB // 128):
                lim = bound[:, j * 128:(j + 1) * 128]
                sj = jnp.minimum(s[:, j * 128:(j + 1) * 128], jnp.concatenate([lim, lim], 0))
                limited.append(sj)
                best = sj if best is None else jnp.maximum(best, sj)
            new = jnp.maximum(old, jnp.max(best, axis=1, keepdims=True))
            shrink = jnp.exp2((old - new) * SCALE)
            shift = new * SCALE
            weights = jnp.concatenate([jnp.exp2(sj * SCALE - shift).astype(jnp.bfloat16) for sj in limited], 1)
            out = jnp.dot(weights, values, preferred_element_type=jnp.float32)
            den[h, rows, :] = den[h, rows, :] * shrink + out[:, HD:]
            acc[h, rows, :] = acc[h, rows, :] * shrink + out[:, :HD]
            top[h, rows, :] = new

        s = score(0)
        for sb in range(4):
            following = score(sb + 1) if sb < 3 else None
            soften(sb, s)
            s = following

        @pl.when(chunk == 5)
        def _():
            for g in range(8):
                rows = pl.ds(g * 256, 256)
                cols = pl.ds(pl.multiple_of((h * 8 + g) * HD, HD), HD)
                stage[:, cols] = (acc[h, rows, :] / den[h, rows, :]).astype(jnp.bfloat16)

        return carry

    lax.fori_loop(0, 24, one, 0)
    send_head(3)

    for copies in (root_sends, own_sends, [q_send], leaf1, leaf2, leaf3, *steps.values()):
        for copy in copies:
            copy.wait_send()
    wait_all(out_sends)
    wait_all(out_locals)


def on_device(queries, seg_keys, seg_values, root_keys, root_values, expansion, root_offsets):
    smem = pl.BlockSpec(memory_space=pltpu.SMEM)
    anywhere = pl.BlockSpec(memory_space=pl.ANY)
    return pl.pallas_call(
        kernel,
        out_shape=jax.ShapeDtypeStruct(queries.shape, jnp.bfloat16),
        in_specs=[smem, smem] + [anywhere] * 5,
        out_specs=anywhere,
        scratch_shapes=[
            pltpu.VMEM((3, 4, 2, 2, 2, 2, 64, 512), jnp.bfloat16),
            pltpu.VMEM((256, 4096), jnp.bfloat16),
            pltpu.VMEM((2, 2, 4, 2, 64, 512), jnp.bfloat16),
            pltpu.VMEM((4, 2, 64, 512), jnp.bfloat16),
            pltpu.VMEM((4, 2, 64, 512), jnp.bfloat16),
            pltpu.VMEM((4, 2048, HD), jnp.float32),
            pltpu.VMEM((4, 2048, HD), jnp.float32),
            pltpu.VMEM((4, 2048, HD), jnp.float32),
            pltpu.VMEM((256, KB), jnp.float32),
            pltpu.VMEM((256, 4096), jnp.bfloat16),
            pltpu.SemaphoreType.DMA((N_COPIES,)),
            pltpu.SemaphoreType.DMA((N_COPIES,)),
            pltpu.SemaphoreType.DMA((N_LOCAL,)),
        ],
        compiler_params=pltpu.CompilerParams(
            collective_id=0, has_side_effects=True, vmem_limit_bytes=60 * 1024 * 1024
        ),
    )(expansion, root_offsets, queries, seg_keys, seg_values, root_keys, root_values)


def solution(mesh):
    return jax.shard_map(
        on_device,
        mesh=mesh,
        in_specs=(
            P(("leaf", "ctx"), None),
            P(("leaf", "ctx"), None),
            P(("leaf", "ctx"), None),
            P("ctx", None),
            P("ctx", None),
            P(),
            P(),
        ),
        out_specs=P(("leaf", "ctx"), None),
        check_vma=False,
    )
```

```python
import functools
import math

import jax
import jax.numpy as jnp
from jax import lax
from jax.experimental import pallas as pl
from jax.experimental.pallas import tpu as pltpu
from jax.sharding import PartitionSpec as P

HQ = 64
KVH = 8
HD = 128
MESH = pl.DeviceIdType.MESH
SCALE = math.log2(math.e) / math.sqrt(HD)
LOW = -1e30

ROOT, OWN, PAR = 0, 1, 2
PARTS = ((0, 80), (80, 96), (176, 80))
ORDERS = ((0, 1, 2), (1, 2, 0), (2, 0, 1))


def order_of(source, part):
    return ORDERS[(part + source) % 3]


N_COPIES = 61
N_LOCAL = 14
KB = 1024
RB = 512


def kernel(expansion, offsets, q_hbm, k_hbm, v_hbm, rk_hbm, rv_hbm, o_hbm,
           kv, qbuf, zbuf, pick, got, acc, top, den, bound, stage, send_sem, recv_sem, local_sem):
    leaf, ctx = lax.axis_index("leaf"), lax.axis_index("ctx")
    z, xh = leaf // 2, leaf % 2
    y, c, k = ctx // 4, (ctx // 2) % 2, ctx % 2
    a, b = ((y + 1) // 2) % 2, y // 2
    d, e = ((z + 1) // 2) % 2, z // 2
    partner = (leaf, ctx + 1 - 2 * k)
    near = (
        (leaf, ctx + 4 - 8 * (y % 2)),
        (leaf, (3 - y) * 4 + c * 2 + k),
        (leaf, ctx + 2 - 4 * c),
    )
    near_d = ((z + 1 - 2 * (z % 2)) * 2 + xh, ctx)
    near_e = ((3 - z) * 2 + xh, ctx)
    near_f = (leaf + 1 - 2 * xh, ctx + 2 - 4 * c)

    barrier = pltpu.get_barrier_semaphore()
    for other in (partner, *near, near_d, near_e, near_f):
        pl.semaphore_signal(barrier, inc=1, device_id=other, device_id_type=MESH)
    pl.semaphore_wait(barrier, 7)

    numbers = iter(range(N_COPIES))

    def remote(src, dst, device):
        number = next(numbers)
        return pltpu.make_async_remote_copy(
            src_ref=src, dst_ref=dst, send_sem=send_sem.at[number], recv_sem=recv_sem.at[number],
            device_id=device, device_id_type=MESH,
        )

    mine512 = pl.ds(pl.multiple_of(k * 512, 128), 512)
    other512 = pl.ds(pl.multiple_of((1 - k) * 512, 128), 512)
    mine4096 = pl.ds(pl.multiple_of(k * 4096, 128), 4096)
    other4096 = pl.ds(pl.multiple_of((1 - k) * 4096, 128), 4096)
    mine128 = pl.ds(pl.multiple_of(k * 128, 128), 128)
    other128 = pl.ds(pl.multiple_of((1 - k) * 128, 128), 128)

    def pair_copies(source, number, arrays):
        sends, locals_ = [], []
        for t, array in enumerate(arrays):
            slot = kv.at[source, a, b, c, t, mine128, :]
            sends.append(remote(array.at[:, other512], slot, partner))
            locals_.append(pltpu.make_async_copy(array.at[:, mine512], slot, local_sem.at[number + t]))
        return sends, locals_

    root_sends, root_locals = pair_copies(ROOT, 0, (rk_hbm, rv_hbm))
    own_sends, own_locals = pair_copies(OWN, 2, (k_hbm, v_hbm))
    q_send = remote(q_hbm.at[:, other4096], qbuf.at[mine128, :], partner)
    q_local = pltpu.make_async_copy(q_hbm.at[:, mine4096], qbuf.at[mine128, :], local_sem.at[8])
    for copy in (*root_sends, *root_locals, *own_sends, *own_locals, q_send, q_local):
        copy.start()

    bits = (a, b, c)

    def block(source, part, where, t=slice(None)):
        first, count = PARTS[part]
        return kv.at[source, where[0], where[1], where[2], t, first:first + count, :]

    both = slice(None)

    def double(source, part, step, second=None):
        order = order_of(source, part)
        where = {dim: both if dim in order[:step] else bits[dim] for dim in range(3)}
        if second is not None:
            where[order[1]] = second
        slot = block(source, part, where)
        return remote(slot, slot, near[order[step]])

    steps = {}
    for source in (ROOT, OWN, PAR):
        for step in (0, 1):
            steps[source, step] = [double(source, part, step) for part in range(3)]
    for source in (OWN, PAR):
        steps[source, 2] = [double(source, p, 2, bits[order_of(source, p)[1]]) for p in range(3)]
        steps[source, 3] = [double(source, p, 2, 1 - bits[order_of(source, p)[1]]) for p in range(3)]

    def shared(part, first, second, last, t=both):
        order = order_of(ROOT, part)
        where = {order[0]: first, order[1]: second, order[2]: last}
        return block(ROOT, part, where, t)

    quarter, round1, round2 = [], [], []
    for part in range(3):
        last = order_of(ROOT, part)[2]
        slot = shared(part, d, e, bits[last])
        quarter.append(remote(slot, slot, near[last]))
        flip = 1 - bits[last]
        for t, (one_way, other_way) in enumerate(((near_d, near_e), (near_e, near_d))):
            slot = shared(part, d, e, flip, t)
            round1.append(remote(slot, slot, one_way))
            slot = shared(part, both, e, flip, t) if t == 0 else shared(part, d, both, flip, t)
            round2.append(remote(slot, slot, other_way))

    def start(copies):
        for copy in copies:
            copy.start()

    def arrive(copies):
        for copy in copies:
            copy.wait_recv()

    def relay(arriving, leaving):
        for before, after in zip(arriving, leaving):
            before.wait_recv()
            after.start()

    def wait_all(copies):
        for copy in copies:
            copy.wait()

    low, high = slice(0, 128), slice(128, 256)
    leaf1 = [
        remote(kv.at[OWN, a, b, c, :, low, :], zbuf.at[d, e, :, low, :], near_d),
        remote(kv.at[OWN, a, b, c, :, high, :], zbuf.at[d, e, :, high, :], near_e),
    ]
    leaf_local = pltpu.make_async_copy(kv.at[OWN, a, b, c], zbuf.at[d, e], local_sem.at[9])
    leaf2 = [
        remote(zbuf.at[:, e, :, low, :], zbuf.at[:, e, :, low, :], near_e),
        remote(zbuf.at[d, :, :, high, :], zbuf.at[d, :, :, high, :], near_d),
    ]
    leaf3 = [remote(pick, got, near_f)]

    arrive(root_sends)
    wait_all(root_locals)
    start(steps[ROOT, 0])
    arrive(own_sends)
    wait_all(own_locals)
    start(leaf1)
    start(steps[OWN, 0])
    leaf_local.start()

    acc[...] = jnp.zeros(acc.shape, jnp.float32)
    den[...] = jnp.zeros(den.shape, jnp.float32)
    top[...] = jnp.full(top.shape, LOW, jnp.float32)

    leaf_local.wait()
    arrive([q_send])
    q_local.wait()

    parent, depth, visible = expansion[0, leaf], expansion[1, leaf], offsets[leaf]
    parent_f = expansion[0, near_f[0]]
    row_pos = y * 512 + c * 256

    def unit_of(group, t):
        zg = group // 2
        return zbuf[((zg + 1) // 2) % 2, zg // 2, t]

    def choose_for_f():
        for t in range(2):
            pick[t] = unit_of(parent_f, t)

    def choose_parent():
        here = (parent % 2) == xh
        for t in range(2):
            kv[PAR, a, b, c, t] = jnp.where(here, unit_of(parent, t), got[t])

    out_cols = [pl.ds(pl.multiple_of((k * 4 + h) * 1024, 128), 1024) for h in range(4)]
    back_cols = [pl.ds(pl.multiple_of(((1 - k) * 4 + h) * 1024, 128), 1024) for h in range(4)]
    out_sends = [
        remote(stage.at[other128, h * 1024:(h + 1) * 1024], o_hbm.at[:, out_cols[h]], partner)
        for h in range(4)
    ]
    out_locals = [
        pltpu.make_async_copy(stage.at[mine128, h * 1024:(h + 1) * 1024], o_hbm.at[:, out_cols[h]], local_sem.at[10 + h])
        for h in range(4)
    ]

    def send_head(h):
        out_sends[h].start()
        out_locals[h].start()

    def do(hooks, it):
        for number, act in hooks.items():
            @pl.when(it == number)
            def _():
                act()

    def piece(part, values):
        first, count = PARTS[part]
        pa, pb, pc = (values[dim] for dim in range(3))
        plane = 2 * pb + pa + pb - 2 * pa * pb
        return first, count, pa, pb, pc, plane * 512 + pc * 256 + first

    def attend(pieces, source, h, kb):
        columns = pl.ds(pl.multiple_of(h * HD, HD), HD)

        @pl.when(h == 0)
        def _():
            if source == ROOT:
                limits = visible
            elif source == OWN:
                limits = lax.broadcasted_iota(jnp.int32, (256, 1), 0) + row_pos + 1
            else:
                limits = jnp.where(depth > 0, 4096, 0)
            column = lax.broadcasted_iota(jnp.int32, (1, kb), 1)
            base, at = None, 0
            for first, count, _, _, _, position in pieces:
                here = position - at + column
                base = here if base is None else jnp.where(column >= at, here, base)
                at += count
            bound[:, :kb] = jnp.broadcast_to(jnp.where(base < limits, 1e38, LOW), (256, kb))

        def gather(t):
            return jnp.concatenate(
                [kv[source, pa, pb, pc, t, first:first + count, columns] for first, count, pa, pb, pc, _ in pieces], 0
            )

        keys = gather(0)
        values = jnp.concatenate([gather(1), jnp.ones((kb, HD), jnp.bfloat16)], 1)

        def score(sb):
            rows = [
                qbuf[:, pl.ds(pl.multiple_of((h * 8 + 2 * sb + i) * HD, HD), HD)] for i in range(2)
            ]
            return lax.dot_general(
                jnp.concatenate(rows, 0), keys, (((1,), (1,)), ((), ())), preferred_element_type=jnp.float32
            )

        def soften(sb, s):
            rows = pl.ds(sb * RB, RB)
            old = top[h, rows, :]
            limited, best = [], None
            for j in range(kb // 128):
                lim = bound[:, j * 128:(j + 1) * 128]
                sj = jnp.minimum(s[:, j * 128:(j + 1) * 128], jnp.concatenate([lim, lim], 0))
                limited.append(sj)
                best = sj if best is None else jnp.maximum(best, sj)
            new = jnp.maximum(old, jnp.max(best, axis=1, keepdims=True))
            shrink = jnp.exp2((old - new) * SCALE)
            shift = new * SCALE
            weights = jnp.concatenate([jnp.exp2(sj * SCALE - shift).astype(jnp.bfloat16) for sj in limited], 1)
            out = jnp.dot(weights, values, preferred_element_type=jnp.float32)
            den[h, rows, :] = den[h, rows, :] * shrink + out[:, HD:]
            acc[h, rows, :] = acc[h, rows, :] * shrink + out[:, :HD]
            top[h, rows, :] = new

        s = score(0)
        for sb in range(4):
            following = score(sb + 1) if sb < 3 else None
            soften(sb, s)
            s = following

    def pieces_of(source, firsts, seconds, last):
        pieces = []
        for part in range(3):
            order = order_of(source, part)
            for first in firsts:
                for second in seconds:
                    own = {dim: bits[dim] for dim in range(3)}
                    values = {
                        order[0]: first,
                        order[1]: second if isinstance(second, int) else (own[order[1]] + second[0]) % 2,
                        order[2]: (own[order[2]] + last) % 2,
                    }
                    pieces.append(piece(part, values))
        return pieces

    def finish(h):
        for g in range(8):
            rows = pl.ds(g * 256, 256)
            cols = pl.ds(pl.multiple_of((h * 8 + g) * HD, HD), HD)
            stage[:, cols] = (acc[h, rows, :] / den[h, rows, :]).astype(jnp.bfloat16)

    def halves(source, last, hooks):
        def one(h, carry):
            do(hooks, h)
            attend(pieces_of(source, (0, 1), (0, 1), last), source, h, 1024)
            return carry

        lax.fori_loop(0, 4, one, 0)

    def quarters(source, last, hooks, final=False):
        def one(it, carry):
            do(hooks, it)
            h = it % 4
            attend(pieces_of(source, (0, 1), ((it // 4,),), last), source, h, 512)
            if final:
                @pl.when(it >= 4)
                def _():
                    finish(h)
            return carry

        lax.fori_loop(0, 8, one, 0)

    quarters(ROOT, 0, {
        0: lambda: relay(steps[ROOT, 0], steps[ROOT, 1]),
        1: lambda: relay(leaf1, leaf2),
        2: lambda: relay(steps[OWN, 0], steps[OWN, 1]),
        4: lambda: relay(steps[ROOT, 1], quarter),
        6: lambda: (arrive(leaf2), choose_for_f()),
        7: lambda: start(leaf3),
    })
    halves(OWN, 0, {
        0: lambda: (relay(steps[OWN, 1], steps[OWN, 2]), start(steps[OWN, 3])),
        1: lambda: (arrive(quarter), start(round1)),
        3: lambda: (arrive(round1), start(round2)),
    })
    quarters(OWN, 1, {
        0: lambda: arrive(steps[OWN, 2]),
        1: lambda: (arrive(leaf3), choose_parent()),
        2: lambda: start(steps[PAR, 0]),
        4: lambda: arrive(steps[OWN, 3]),
        6: lambda: relay(steps[PAR, 0], steps[PAR, 1]),
    })
    halves(ROOT, 1, {
        0: lambda: arrive(round2),
        2: lambda: (relay(steps[PAR, 1], steps[PAR, 2]), start(steps[PAR, 3])),
    })
    halves(PAR, 0, {})
    quarters(PAR, 1, {
        0: lambda: arrive(steps[PAR, 2]),
        4: lambda: arrive(steps[PAR, 3]),
        5: lambda: send_head(0),
        6: lambda: send_head(1),
        7: lambda: send_head(2),
    }, final=True)
    send_head(3)

    for copies in (
        root_sends, own_sends, [q_send], leaf1, leaf2, leaf3, quarter, round1, round2, *steps.values()
    ):
        for copy in copies:
            copy.wait_send()
    wait_all(out_sends)
    wait_all(out_locals)


def on_device(queries, seg_keys, seg_values, root_keys, root_values, expansion, root_offsets):
    smem = pl.BlockSpec(memory_space=pltpu.SMEM)
    anywhere = pl.BlockSpec(memory_space=pl.ANY)
    return pl.pallas_call(
        kernel,
        out_shape=jax.ShapeDtypeStruct(queries.shape, jnp.bfloat16),
        in_specs=[smem, smem] + [anywhere] * 5,
        out_specs=anywhere,
        scratch_shapes=[
            pltpu.VMEM((3, 2, 2, 2, 2, 256, 512), jnp.bfloat16),
            pltpu.VMEM((256, 4096), jnp.bfloat16),
            pltpu.VMEM((2, 2, 2, 256, 512), jnp.bfloat16),
            pltpu.VMEM((2, 256, 512), jnp.bfloat16),
            pltpu.VMEM((2, 256, 512), jnp.bfloat16),
            pltpu.VMEM((4, 2048, HD), jnp.float32),
            pltpu.VMEM((4, 2048, HD), jnp.float32),
            pltpu.VMEM((4, 2048, HD), jnp.float32),
            pltpu.VMEM((256, KB), jnp.float32),
            pltpu.VMEM((256, 4096), jnp.bfloat16),
            pltpu.SemaphoreType.DMA((N_COPIES,)),
            pltpu.SemaphoreType.DMA((N_COPIES,)),
            pltpu.SemaphoreType.DMA((N_LOCAL,)),
        ],
        compiler_params=pltpu.CompilerParams(
            collective_id=0, has_side_effects=True, vmem_limit_bytes=60 * 1024 * 1024
        ),
    )(expansion, root_offsets, queries, seg_keys, seg_values, root_keys, root_values)


def solution(mesh):
    return jax.shard_map(
        on_device,
        mesh=mesh,
        in_specs=(
            P(("leaf", "ctx"), None),
            P(("leaf", "ctx"), None),
            P(("leaf", "ctx"), None),
            P("ctx", None),
            P("ctx", None),
            P(),
            P(),
        ),
        out_specs=P(("leaf", "ctx"), None),
        check_vma=False,
    )
```

```python
import functools
import math

import jax
import jax.numpy as jnp
from jax import lax
from jax.experimental import pallas as pl
from jax.experimental.pallas import tpu as pltpu
from jax.sharding import PartitionSpec as P

HQ = 64
KVH = 8
HD = 128
MESH = pl.DeviceIdType.MESH
SCALE = math.log2(math.e) / math.sqrt(HD)
LOW = -1e30

ROOT, OWN, PAR = 0, 1, 2
PARTS = ((0, 80), (80, 96), (176, 80))
ORDERS = ((0, 1, 2), (1, 2, 0), (2, 0, 1))


def order_of(source, part):
    return ORDERS[(part + source) % 3]


N_COPIES = 61
N_LOCAL = 14


def kernel(expansion, offsets, q_hbm, k_hbm, v_hbm, rk_hbm, rv_hbm, o_hbm,
           kv, qbuf, zbuf, pick, got, acc, top, den, bound, stage, send_sem, recv_sem, local_sem):
    leaf, ctx = lax.axis_index("leaf"), lax.axis_index("ctx")
    z, xh = leaf // 2, leaf % 2
    y, c, k = ctx // 4, (ctx // 2) % 2, ctx % 2
    a, b = ((y + 1) // 2) % 2, y // 2
    d, e = ((z + 1) // 2) % 2, z // 2
    partner = (leaf, ctx + 1 - 2 * k)
    near = (
        (leaf, ctx + 4 - 8 * (y % 2)),
        (leaf, (3 - y) * 4 + c * 2 + k),
        (leaf, ctx + 2 - 4 * c),
    )
    near_d = ((z + 1 - 2 * (z % 2)) * 2 + xh, ctx)
    near_e = ((3 - z) * 2 + xh, ctx)
    near_f = (leaf + 1 - 2 * xh, ctx + 2 - 4 * c)

    barrier = pltpu.get_barrier_semaphore()
    for other in (partner, *near, near_d, near_e, near_f):
        pl.semaphore_signal(barrier, inc=1, device_id=other, device_id_type=MESH)
    pl.semaphore_wait(barrier, 7)

    numbers = iter(range(N_COPIES))

    def remote(src, dst, device):
        number = next(numbers)
        return pltpu.make_async_remote_copy(
            src_ref=src, dst_ref=dst, send_sem=send_sem.at[number], recv_sem=recv_sem.at[number],
            device_id=device, device_id_type=MESH,
        )

    mine512 = pl.ds(pl.multiple_of(k * 512, 128), 512)
    other512 = pl.ds(pl.multiple_of((1 - k) * 512, 128), 512)
    mine4096 = pl.ds(pl.multiple_of(k * 4096, 128), 4096)
    other4096 = pl.ds(pl.multiple_of((1 - k) * 4096, 128), 4096)
    mine128 = pl.ds(pl.multiple_of(k * 128, 128), 128)
    other128 = pl.ds(pl.multiple_of((1 - k) * 128, 128), 128)

    def pair_copies(source, number, arrays):
        sends, locals_ = [], []
        for t, array in enumerate(arrays):
            slot = kv.at[source, a, b, c, t, mine128, :]
            sends.append(remote(array.at[:, other512], slot, partner))
            locals_.append(pltpu.make_async_copy(array.at[:, mine512], slot, local_sem.at[number + t]))
        return sends, locals_

    root_sends, root_locals = pair_copies(ROOT, 0, (rk_hbm, rv_hbm))
    own_sends, own_locals = pair_copies(OWN, 2, (k_hbm, v_hbm))
    q_send = remote(q_hbm.at[:, other4096], qbuf.at[mine128, :], partner)
    q_local = pltpu.make_async_copy(q_hbm.at[:, mine4096], qbuf.at[mine128, :], local_sem.at[8])
    for copy in (*root_sends, *root_locals, *own_sends, *own_locals, q_send, q_local):
        copy.start()

    bits = (a, b, c)

    def block(source, part, where, t=slice(None)):
        first, count = PARTS[part]
        return kv.at[source, where[0], where[1], where[2], t, first:first + count, :]

    both = slice(None)

    def double(source, part, step, second=None):
        order = order_of(source, part)
        where = {dim: both if dim in order[:step] else bits[dim] for dim in range(3)}
        if second is not None:
            where[order[1]] = second
        slot = block(source, part, where)
        return remote(slot, slot, near[order[step]])

    steps = {}
    for source in (ROOT, OWN, PAR):
        for step in (0, 1):
            steps[source, step] = [double(source, part, step) for part in range(3)]
    for source in (OWN, PAR):
        steps[source, 2] = [double(source, p, 2, bits[order_of(source, p)[1]]) for p in range(3)]
        steps[source, 3] = [double(source, p, 2, 1 - bits[order_of(source, p)[1]]) for p in range(3)]

    def shared(part, first, second, last, t=both):
        order = order_of(ROOT, part)
        where = {order[0]: first, order[1]: second, order[2]: last}
        return block(ROOT, part, where, t)

    quarter, round1, round2 = [], [], []
    for part in range(3):
        last = order_of(ROOT, part)[2]
        slot = shared(part, d, e, bits[last])
        quarter.append(remote(slot, slot, near[last]))
        flip = 1 - bits[last]
        for t, (one_way, other_way) in enumerate(((near_d, near_e), (near_e, near_d))):
            slot = shared(part, d, e, flip, t)
            round1.append(remote(slot, slot, one_way))
            slot = shared(part, both, e, flip, t) if t == 0 else shared(part, d, both, flip, t)
            round2.append(remote(slot, slot, other_way))

    def start(copies):
        for copy in copies:
            copy.start()

    def arrive(copies):
        for copy in copies:
            copy.wait_recv()

    def relay(arriving, leaving):
        for before, after in zip(arriving, leaving):
            before.wait_recv()
            after.start()

    def wait_all(copies):
        for copy in copies:
            copy.wait()

    low, high = slice(0, 128), slice(128, 256)
    leaf1 = [
        remote(kv.at[OWN, a, b, c, :, low, :], zbuf.at[d, e, :, low, :], near_d),
        remote(kv.at[OWN, a, b, c, :, high, :], zbuf.at[d, e, :, high, :], near_e),
    ]
    leaf_local = pltpu.make_async_copy(kv.at[OWN, a, b, c], zbuf.at[d, e], local_sem.at[9])
    leaf2 = [
        remote(zbuf.at[:, e, :, low, :], zbuf.at[:, e, :, low, :], near_e),
        remote(zbuf.at[d, :, :, high, :], zbuf.at[d, :, :, high, :], near_d),
    ]
    leaf3 = [remote(pick, got, near_f)]

    arrive(root_sends)
    wait_all(root_locals)
    start(steps[ROOT, 0])
    arrive(own_sends)
    wait_all(own_locals)
    start(leaf1)
    start(steps[OWN, 0])
    leaf_local.start()

    acc[...] = jnp.zeros(acc.shape, jnp.float32)
    den[...] = jnp.zeros(den.shape, jnp.float32)
    top[...] = jnp.full(top.shape, LOW, jnp.float32)

    leaf_local.wait()
    arrive([q_send])
    q_local.wait()

    parent, depth, visible = expansion[0, leaf], expansion[1, leaf], offsets[leaf]
    parent_f = expansion[0, near_f[0]]
    row_pos = y * 512 + c * 256

    def unit_of(group, t):
        zg = group // 2
        return zbuf[((zg + 1) // 2) % 2, zg // 2, t]

    def choose_for_f():
        for t in range(2):
            pick[t] = unit_of(parent_f, t)

    def choose_parent():
        here = (parent % 2) == xh
        for t in range(2):
            kv[PAR, a, b, c, t] = jnp.where(here, unit_of(parent, t), got[t])

    out_cols = [pl.ds(pl.multiple_of((k * 4 + h) * 1024, 128), 1024) for h in range(4)]
    back_cols = [pl.ds(pl.multiple_of(((1 - k) * 4 + h) * 1024, 128), 1024) for h in range(4)]
    out_sends = [
        remote(stage.at[other128, h * 1024:(h + 1) * 1024], o_hbm.at[:, out_cols[h]], partner)
        for h in range(4)
    ]
    out_locals = [
        pltpu.make_async_copy(stage.at[mine128, h * 1024:(h + 1) * 1024], o_hbm.at[:, out_cols[h]], local_sem.at[10 + h])
        for h in range(4)
    ]

    def send_head(h):
        out_sends[h].start()
        out_locals[h].start()

    def do(hooks, it):
        for number, act in hooks.items():
            @pl.when(it == number)
            def _():
                act()

    def piece(part, values):
        first, count = PARTS[part]
        pa, pb, pc = (values[dim] for dim in range(3))
        plane = 2 * pb + pa + pb - 2 * pa * pb
        return first, count, pa, pb, pc, plane * 512 + pc * 256 + first

    def attend(pieces, source, h, kb):
        rb = kb
        heads = rb // 256
        columns = pl.ds(pl.multiple_of(h * HD, HD), HD)

        @pl.when(h == 0)
        def _():
            if source == ROOT:
                limits = visible
            elif source == OWN:
                limits = lax.broadcasted_iota(jnp.int32, (256, 1), 0) + row_pos + 1
            else:
                limits = jnp.where(depth > 0, 4096, 0)
            column = lax.broadcasted_iota(jnp.int32, (1, kb), 1)
            base, at = None, 0
            for first, count, _, _, _, position in pieces:
                here = position - at + column
                base = here if base is None else jnp.where(column >= at, here, base)
                at += count
            bound[:, :kb] = jnp.broadcast_to(jnp.where(base < limits, 1e38, LOW), (256, kb))

        def gather(t):
            return jnp.concatenate(
                [kv[source, pa, pb, pc, t, first:first + count, columns] for first, count, pa, pb, pc, _ in pieces], 0
            )

        keys = gather(0)
        values = jnp.concatenate([gather(1), jnp.ones((kb, HD), jnp.bfloat16)], 1)

        def score(sb):
            rows = [
                qbuf[:, pl.ds(pl.multiple_of((h * 8 + heads * sb + i) * HD, HD), HD)] for i in range(heads)
            ]
            return lax.dot_general(
                jnp.concatenate(rows, 0), keys, (((1,), (1,)), ((), ())), preferred_element_type=jnp.float32
            )

        def soften(sb, s):
            rows = pl.ds(sb * rb, rb)
            old = top[h, rows, :]
            limited, best = [], None
            for j in range(kb // 128):
                lim = bound[:, j * 128:(j + 1) * 128]
                sj = jnp.minimum(s[:, j * 128:(j + 1) * 128], jnp.concatenate([lim] * heads, 0))
                limited.append(sj)
                best = sj if best is None else jnp.maximum(best, sj)
            new = jnp.maximum(old, jnp.max(best, axis=1, keepdims=True))
            shrink = jnp.exp2((old - new) * SCALE)
            shift = new * SCALE
            weights = jnp.concatenate([jnp.exp2(sj * SCALE - shift).astype(jnp.bfloat16) for sj in limited], 1)
            out = jnp.dot(weights, values, preferred_element_type=jnp.float32)
            den[h, rows, :] = den[h, rows, :] * shrink + out[:, HD:]
            acc[h, rows, :] = acc[h, rows, :] * shrink + out[:, :HD]
            top[h, rows, :] = new

        s = score(0)
        for sb in range(2048 // rb):
            following = score(sb + 1) if sb + 1 < 2048 // rb else None
            soften(sb, s)
            s = following

    def pieces_of(source, firsts, seconds, last):
        pieces = []
        for part in range(3):
            order = order_of(source, part)
            for first in firsts:
                for second in seconds:
                    own = {dim: bits[dim] for dim in range(3)}
                    values = {
                        order[0]: first,
                        order[1]: second if isinstance(second, int) else (own[order[1]] + second[0]) % 2,
                        order[2]: (own[order[2]] + last) % 2,
                    }
                    pieces.append(piece(part, values))
        return pieces

    def finish(h):
        for g in range(8):
            rows = pl.ds(g * 256, 256)
            cols = pl.ds(pl.multiple_of((h * 8 + g) * HD, HD), HD)
            stage[:, cols] = (acc[h, rows, :] / den[h, rows, :]).astype(jnp.bfloat16)

    def halves(source, last, hooks, final=False):
        def one(h, carry):
            do(hooks, h)
            attend(pieces_of(source, (0, 1), (0, 1), last), source, h, 1024)
            if final:
                finish(h)
            return carry

        lax.fori_loop(0, 4, one, 0)

    def quarters(source, last, hooks):
        def one(it, carry):
            do(hooks, it)
            h = it % 4
            attend(pieces_of(source, (0, 1), ((it // 4,),), last), source, h, 512)
            return carry

        lax.fori_loop(0, 8, one, 0)

    quarters(ROOT, 0, {
        0: lambda: relay(steps[ROOT, 0], steps[ROOT, 1]),
        1: lambda: relay(leaf1, leaf2),
        2: lambda: relay(steps[OWN, 0], steps[OWN, 1]),
        4: lambda: relay(steps[ROOT, 1], quarter),
        6: lambda: (arrive(leaf2), choose_for_f()),
        7: lambda: start(leaf3),
    })
    halves(OWN, 0, {
        0: lambda: (relay(steps[OWN, 1], steps[OWN, 2]), start(steps[OWN, 3])),
        1: lambda: (arrive(quarter), start(round1)),
        3: lambda: (arrive(round1), start(round2)),
    })
    quarters(OWN, 1, {
        0: lambda: arrive(steps[OWN, 2]),
        1: lambda: (arrive(leaf3), choose_parent()),
        2: lambda: start(steps[PAR, 0]),
        4: lambda: arrive(steps[OWN, 3]),
        6: lambda: relay(steps[PAR, 0], steps[PAR, 1]),
    })
    halves(ROOT, 1, {
        0: lambda: arrive(round2),
        2: lambda: (relay(steps[PAR, 1], steps[PAR, 2]), start(steps[PAR, 3])),
    })
    halves(PAR, 0, {})
    halves(PAR, 1, {
        0: lambda: (arrive(steps[PAR, 2]), arrive(steps[PAR, 3])),
        1: lambda: send_head(0),
        2: lambda: send_head(1),
        3: lambda: send_head(2),
    }, final=True)
    send_head(3)

    for copies in (
        root_sends, own_sends, [q_send], leaf1, leaf2, leaf3, quarter, round1, round2, *steps.values()
    ):
        for copy in copies:
            copy.wait_send()
    wait_all(out_sends)
    wait_all(out_locals)


def on_device(queries, seg_keys, seg_values, root_keys, root_values, expansion, root_offsets):
    smem = pl.BlockSpec(memory_space=pltpu.SMEM)
    anywhere = pl.BlockSpec(memory_space=pl.ANY)
    return pl.pallas_call(
        kernel,
        out_shape=jax.ShapeDtypeStruct(queries.shape, jnp.bfloat16),
        in_specs=[smem, smem] + [anywhere] * 5,
        out_specs=anywhere,
        scratch_shapes=[
            pltpu.VMEM((3, 2, 2, 2, 2, 256, 512), jnp.bfloat16),
            pltpu.VMEM((256, 4096), jnp.bfloat16),
            pltpu.VMEM((2, 2, 2, 256, 512), jnp.bfloat16),
            pltpu.VMEM((2, 256, 512), jnp.bfloat16),
            pltpu.VMEM((2, 256, 512), jnp.bfloat16),
            pltpu.VMEM((4, 2048, HD), jnp.float32),
            pltpu.VMEM((4, 2048, HD), jnp.float32),
            pltpu.VMEM((4, 2048, HD), jnp.float32),
            pltpu.VMEM((256, 1024), jnp.float32),
            pltpu.VMEM((256, 4096), jnp.bfloat16),
            pltpu.SemaphoreType.DMA((N_COPIES,)),
            pltpu.SemaphoreType.DMA((N_COPIES,)),
            pltpu.SemaphoreType.DMA((N_LOCAL,)),
        ],
        compiler_params=pltpu.CompilerParams(
            collective_id=0, has_side_effects=True, vmem_limit_bytes=60 * 1024 * 1024
        ),
    )(expansion, root_offsets, queries, seg_keys, seg_values, root_keys, root_values)


def solution(mesh):
    return jax.shard_map(
        on_device,
        mesh=mesh,
        in_specs=(
            P(("leaf", "ctx"), None),
            P(("leaf", "ctx"), None),
            P(("leaf", "ctx"), None),
            P("ctx", None),
            P("ctx", None),
            P(),
            P(),
        ),
        out_specs=P(("leaf", "ctx"), None),
        check_vma=False,
    )
```

```python
import functools
import math

import jax
import jax.numpy as jnp
from jax import lax
from jax.experimental import pallas as pl
from jax.experimental.pallas import tpu as pltpu
from jax.sharding import PartitionSpec as P

HQ = 64
KVH = 8
HD = 128
MESH = pl.DeviceIdType.MESH
SCALE = math.log2(math.e) / math.sqrt(HD)
LOW = -1e30

ROOT, OWN, PAR = 0, 1, 2
PARTS = ((0, 80), (80, 96), (176, 80))
ORDERS = ((0, 1, 2), (1, 2, 0), (2, 0, 1))


def order_of(source, part):
    return ORDERS[(part + source) % 3]


N_COPIES = 61
N_LOCAL = 14


def kernel(expansion, offsets, q_hbm, k_hbm, v_hbm, rk_hbm, rv_hbm, o_hbm,
           kv, qbuf, zbuf, pick, got, acc, top, den, bound, stage, send_sem, recv_sem, local_sem):
    leaf, ctx = lax.axis_index("leaf"), lax.axis_index("ctx")
    z, xh = leaf // 2, leaf % 2
    y, c, k = ctx // 4, (ctx // 2) % 2, ctx % 2
    a, b = ((y + 1) // 2) % 2, y // 2
    d, e = ((z + 1) // 2) % 2, z // 2
    partner = (leaf, ctx + 1 - 2 * k)
    near = (
        (leaf, ctx + 4 - 8 * (y % 2)),
        (leaf, (3 - y) * 4 + c * 2 + k),
        (leaf, ctx + 2 - 4 * c),
    )
    near_d = ((z + 1 - 2 * (z % 2)) * 2 + xh, ctx)
    near_e = ((3 - z) * 2 + xh, ctx)
    near_f = (leaf + 1 - 2 * xh, ctx + 2 - 4 * c)

    barrier = pltpu.get_barrier_semaphore()
    for other in (partner, *near, near_d, near_e, near_f):
        pl.semaphore_signal(barrier, inc=1, device_id=other, device_id_type=MESH)
    pl.semaphore_wait(barrier, 7)

    numbers = iter(range(N_COPIES))

    def remote(src, dst, device):
        number = next(numbers)
        return pltpu.make_async_remote_copy(
            src_ref=src, dst_ref=dst, send_sem=send_sem.at[number], recv_sem=recv_sem.at[number],
            device_id=device, device_id_type=MESH,
        )

    mine512 = pl.ds(pl.multiple_of(k * 512, 128), 512)
    other512 = pl.ds(pl.multiple_of((1 - k) * 512, 128), 512)
    mine4096 = pl.ds(pl.multiple_of(k * 4096, 128), 4096)
    other4096 = pl.ds(pl.multiple_of((1 - k) * 4096, 128), 4096)
    mine128 = pl.ds(pl.multiple_of(k * 128, 128), 128)
    other128 = pl.ds(pl.multiple_of((1 - k) * 128, 128), 128)

    def pair_copies(source, number, arrays):
        sends, locals_ = [], []
        for t, array in enumerate(arrays):
            slot = kv.at[source, a, b, c, t, mine128, :]
            sends.append(remote(array.at[:, other512], slot, partner))
            locals_.append(pltpu.make_async_copy(array.at[:, mine512], slot, local_sem.at[number + t]))
        return sends, locals_

    root_sends, root_locals = pair_copies(ROOT, 0, (rk_hbm, rv_hbm))
    own_sends, own_locals = pair_copies(OWN, 2, (k_hbm, v_hbm))
    q_send = remote(q_hbm.at[:, other4096], qbuf.at[mine128, :], partner)
    q_local = pltpu.make_async_copy(q_hbm.at[:, mine4096], qbuf.at[mine128, :], local_sem.at[8])
    for copy in (*root_sends, *root_locals, *own_sends, *own_locals, q_send, q_local):
        copy.start()

    bits = (a, b, c)

    def block(source, part, where, t=slice(None)):
        first, count = PARTS[part]
        return kv.at[source, where[0], where[1], where[2], t, first:first + count, :]

    both = slice(None)

    def toward(source, dim):
        return near_f if source == ROOT and dim == 2 else near[dim]

    def double(source, part, step, second=None):
        order = order_of(source, part)
        where = {dim: both if dim in order[:step] else bits[dim] for dim in range(3)}
        if second is not None:
            where[order[1]] = second
        slot = block(source, part, where)
        return remote(slot, slot, toward(source, order[step]))

    steps = {}
    for source in (ROOT, OWN, PAR):
        for step in (0, 1):
            steps[source, step] = [double(source, part, step) for part in range(3)]
    for source in (OWN, PAR):
        steps[source, 2] = [double(source, p, 2, bits[order_of(source, p)[1]]) for p in range(3)]
        steps[source, 3] = [double(source, p, 2, 1 - bits[order_of(source, p)[1]]) for p in range(3)]

    def shared(part, first, second, last, t=both):
        order = order_of(ROOT, part)
        where = {order[0]: first, order[1]: second, order[2]: last}
        return block(ROOT, part, where, t)

    quarter, round1, round2 = [], [], []
    for part in range(3):
        last = order_of(ROOT, part)[2]
        slot = shared(part, d, e, bits[last])
        quarter.append(remote(slot, slot, toward(ROOT, last)))
        flip = 1 - bits[last]
        for t, (one_way, other_way) in enumerate(((near_d, near_e), (near_e, near_d))):
            slot = shared(part, d, e, flip, t)
            round1.append(remote(slot, slot, one_way))
            slot = shared(part, both, e, flip, t) if t == 0 else shared(part, d, both, flip, t)
            round2.append(remote(slot, slot, other_way))

    def start(copies):
        for copy in copies:
            copy.start()

    def arrive(copies):
        for copy in copies:
            copy.wait_recv()

    def relay(arriving, leaving):
        for before, after in zip(arriving, leaving):
            before.wait_recv()
            after.start()

    def wait_all(copies):
        for copy in copies:
            copy.wait()

    low, high = slice(0, 128), slice(128, 256)
    leaf1 = [
        remote(kv.at[OWN, a, b, c, :, low, :], zbuf.at[d, e, :, low, :], near_d),
        remote(kv.at[OWN, a, b, c, :, high, :], zbuf.at[d, e, :, high, :], near_e),
    ]
    leaf_local = pltpu.make_async_copy(kv.at[OWN, a, b, c], zbuf.at[d, e], local_sem.at[9])
    leaf2 = [
        remote(zbuf.at[:, e, :, low, :], zbuf.at[:, e, :, low, :], near_e),
        remote(zbuf.at[d, :, :, high, :], zbuf.at[d, :, :, high, :], near_d),
    ]
    leaf3 = [remote(pick, got, near_f)]

    arrive(root_sends)
    wait_all(root_locals)
    start(steps[ROOT, 0])
    arrive(own_sends)
    wait_all(own_locals)
    start(leaf1)
    start(steps[OWN, 0])
    leaf_local.start()

    acc[...] = jnp.zeros(acc.shape, jnp.float32)
    den[...] = jnp.zeros(den.shape, jnp.float32)
    top[...] = jnp.full(top.shape, LOW, jnp.float32)

    leaf_local.wait()
    arrive([q_send])
    q_local.wait()

    parent, depth, visible = expansion[0, leaf], expansion[1, leaf], offsets[leaf]
    parent_f = expansion[0, near_f[0]]
    row_pos = y * 512 + c * 256

    def unit_of(group, t):
        zg = group // 2
        return zbuf[((zg + 1) // 2) % 2, zg // 2, t]

    def choose_for_f():
        for t in range(2):
            pick[t] = unit_of(parent_f, t)

    def choose_parent():
        here = (parent % 2) == xh
        for t in range(2):
            kv[PAR, a, b, c, t] = jnp.where(here, unit_of(parent, t), got[t])

    out_cols = [pl.ds(pl.multiple_of((k * 4 + h) * 1024, 128), 1024) for h in range(4)]
    back_cols = [pl.ds(pl.multiple_of(((1 - k) * 4 + h) * 1024, 128), 1024) for h in range(4)]
    out_sends = [
        remote(stage.at[other128, h * 1024:(h + 1) * 1024], o_hbm.at[:, out_cols[h]], partner)
        for h in range(4)
    ]
    out_locals = [
        pltpu.make_async_copy(stage.at[mine128, h * 1024:(h + 1) * 1024], o_hbm.at[:, out_cols[h]], local_sem.at[10 + h])
        for h in range(4)
    ]

    def send_head(h):
        out_sends[h].start()
        out_locals[h].start()

    def do(hooks, it):
        for number, act in hooks.items():
            @pl.when(it == number)
            def _():
                act()

    def piece(part, values):
        first, count = PARTS[part]
        pa, pb, pc = (values[dim] for dim in range(3))
        plane = 2 * pb + pa + pb - 2 * pa * pb
        return first, count, pa, pb, pc, plane * 512 + pc * 256 + first

    def attend(pieces, source, h, kb):
        rb = kb
        heads = rb // 256
        columns = pl.ds(pl.multiple_of(h * HD, HD), HD)

        @pl.when(h == 0)
        def _():
            if source == ROOT:
                limits = visible
            elif source == OWN:
                limits = lax.broadcasted_iota(jnp.int32, (256, 1), 0) + row_pos + 1
            else:
                limits = jnp.where(depth > 0, 4096, 0)
            column = lax.broadcasted_iota(jnp.int32, (1, kb), 1)
            base, at = None, 0
            for first, count, _, _, _, position in pieces:
                here = position - at + column
                base = here if base is None else jnp.where(column >= at, here, base)
                at += count
            bound[:, :kb] = jnp.broadcast_to(jnp.where(base < limits, 1e38, LOW), (256, kb))

        def gather(t):
            return jnp.concatenate(
                [kv[source, pa, pb, pc, t, first:first + count, columns] for first, count, pa, pb, pc, _ in pieces], 0
            )

        keys = gather(0)
        values = jnp.concatenate([gather(1), jnp.ones((kb, HD), jnp.bfloat16)], 1)

        def score(sb):
            rows = [
                qbuf[:, pl.ds(pl.multiple_of((h * 8 + heads * sb + i) * HD, HD), HD)] for i in range(heads)
            ]
            return lax.dot_general(
                jnp.concatenate(rows, 0), keys, (((1,), (1,)), ((), ())), preferred_element_type=jnp.float32
            )

        def soften(sb, s):
            rows = pl.ds(sb * rb, rb)
            old = top[h, rows, :]
            limited, best = [], None
            for j in range(kb // 128):
                lim = bound[:, j * 128:(j + 1) * 128]
                sj = jnp.minimum(s[:, j * 128:(j + 1) * 128], jnp.concatenate([lim] * heads, 0))
                limited.append(sj)
                best = sj if best is None else jnp.maximum(best, sj)
            new = jnp.maximum(old, jnp.max(best, axis=1, keepdims=True))
            shrink = jnp.exp2((old - new) * SCALE)
            shift = new * SCALE
            weights = jnp.concatenate([jnp.exp2(sj * SCALE - shift).astype(jnp.bfloat16) for sj in limited], 1)
            out = jnp.dot(weights, values, preferred_element_type=jnp.float32)
            den[h, rows, :] = den[h, rows, :] * shrink + out[:, HD:]
            acc[h, rows, :] = acc[h, rows, :] * shrink + out[:, :HD]
            top[h, rows, :] = new

        s = score(0)
        for sb in range(2048 // rb):
            following = score(sb + 1) if sb + 1 < 2048 // rb else None
            soften(sb, s)
            s = following

    def pieces_of(source, firsts, seconds, last):
        pieces = []
        for part in range(3):
            order = order_of(source, part)
            for first in firsts:
                for second in seconds:
                    own = {dim: bits[dim] for dim in range(3)}
                    values = {
                        order[0]: first,
                        order[1]: second if isinstance(second, int) else (own[order[1]] + second[0]) % 2,
                        order[2]: (own[order[2]] + last) % 2,
                    }
                    pieces.append(piece(part, values))
        return pieces

    def finish(h):
        for g in range(8):
            rows = pl.ds(g * 256, 256)
            cols = pl.ds(pl.multiple_of((h * 8 + g) * HD, HD), HD)
            stage[:, cols] = (acc[h, rows, :] / den[h, rows, :]).astype(jnp.bfloat16)

    def halves(source, last, hooks, final=False):
        def one(h, carry):
            do(hooks, h)
            attend(pieces_of(source, (0, 1), (0, 1), last), source, h, 1024)
            if final:
                finish(h)
            return carry

        lax.fori_loop(0, 4, one, 0)

    def quarters(source, last, hooks):
        def one(it, carry):
            do(hooks, it)
            h = it % 4
            attend(pieces_of(source, (0, 1), ((it // 4,),), last), source, h, 512)
            return carry

        lax.fori_loop(0, 8, one, 0)

    quarters(ROOT, 0, {
        0: lambda: relay(steps[ROOT, 0], steps[ROOT, 1]),
        1: lambda: relay(leaf1, leaf2),
        2: lambda: relay(steps[OWN, 0], steps[OWN, 1]),
        4: lambda: relay(steps[ROOT, 1], quarter),
        6: lambda: (arrive(leaf2), choose_for_f()),
        7: lambda: start(leaf3),
    })
    halves(OWN, 0, {
        0: lambda: (relay(steps[OWN, 1], steps[OWN, 2]), start(steps[OWN, 3])),
        1: lambda: (arrive(quarter), start(round1)),
        3: lambda: (arrive(round1), start(round2)),
    })
    quarters(OWN, 1, {
        0: lambda: arrive(steps[OWN, 2]),
        1: lambda: (arrive(leaf3), choose_parent()),
        2: lambda: start(steps[PAR, 0]),
        4: lambda: arrive(steps[OWN, 3]),
        6: lambda: relay(steps[PAR, 0], steps[PAR, 1]),
    })
    halves(ROOT, 1, {
        0: lambda: arrive(round2),
        2: lambda: (relay(steps[PAR, 1], steps[PAR, 2]), start(steps[PAR, 3])),
    })
    halves(PAR, 0, {})
    halves(PAR, 1, {
        0: lambda: (arrive(steps[PAR, 2]), arrive(steps[PAR, 3])),
        1: lambda: send_head(0),
        2: lambda: send_head(1),
        3: lambda: send_head(2),
    }, final=True)
    send_head(3)

    for copies in (
        root_sends, own_sends, [q_send], leaf1, leaf2, leaf3, quarter, round1, round2, *steps.values()
    ):
        for copy in copies:
            copy.wait_send()
    wait_all(out_sends)
    wait_all(out_locals)


def on_device(queries, seg_keys, seg_values, root_keys, root_values, expansion, root_offsets):
    smem = pl.BlockSpec(memory_space=pltpu.SMEM)
    anywhere = pl.BlockSpec(memory_space=pl.ANY)
    return pl.pallas_call(
        kernel,
        out_shape=jax.ShapeDtypeStruct(queries.shape, jnp.bfloat16),
        in_specs=[smem, smem] + [anywhere] * 5,
        out_specs=anywhere,
        scratch_shapes=[
            pltpu.VMEM((3, 2, 2, 2, 2, 256, 512), jnp.bfloat16),
            pltpu.VMEM((256, 4096), jnp.bfloat16),
            pltpu.VMEM((2, 2, 2, 256, 512), jnp.bfloat16),
            pltpu.VMEM((2, 256, 512), jnp.bfloat16),
            pltpu.VMEM((2, 256, 512), jnp.bfloat16),
            pltpu.VMEM((4, 2048, HD), jnp.float32),
            pltpu.VMEM((4, 2048, HD), jnp.float32),
            pltpu.VMEM((4, 2048, HD), jnp.float32),
            pltpu.VMEM((256, 1024), jnp.float32),
            pltpu.VMEM((256, 4096), jnp.bfloat16),
            pltpu.SemaphoreType.DMA((N_COPIES,)),
            pltpu.SemaphoreType.DMA((N_COPIES,)),
            pltpu.SemaphoreType.DMA((N_LOCAL,)),
        ],
        compiler_params=pltpu.CompilerParams(
            collective_id=0, has_side_effects=True, vmem_limit_bytes=60 * 1024 * 1024
        ),
    )(expansion, root_offsets, queries, seg_keys, seg_values, root_keys, root_values)


def solution(mesh):
    return jax.shard_map(
        on_device,
        mesh=mesh,
        in_specs=(
            P(("leaf", "ctx"), None),
            P(("leaf", "ctx"), None),
            P(("leaf", "ctx"), None),
            P("ctx", None),
            P("ctx", None),
            P(),
            P(),
        ),
        out_specs=P(("leaf", "ctx"), None),
        check_vma=False,
    )
```
